32 devices in a mesh: grp: 2 (over y), sx: 16 (over z, x, core).
Axes of the slice: x: 2, y: 2, z: 4, core: 2. Of those that a mesh axis runs over, the one named last changes fastest.
Arguments:
- features: bfloat16 [8, 64, 64, 4, 64], P('grp', 'sx'), parts along dimension 0, may hold values from -28 to 28
- weight: bfloat16 [3, 3, 3, 64, 128], replicated, may hold values from -0.15625 to 0.15625
- gain: float32 [128], replicated, may hold values from 0.1 to 1.9
- shift: float32 [128], replicated, may hold values from -3 to 3
- cotangent: bfloat16 [256, 32, 2, 128], P(('grp', 'sx')), parts along dimension 0, may hold values from -25 to 25
Outputs:
- regrouped: bfloat16 [256, 32, 2, 128], P(('grp', 'sx')), parts along dimension 0
- grad_features: bfloat16 [8, 64, 64, 4, 64], P('grp', 'sx'), parts along dimension 0
- grad_weight: float32 [6, 3, 3, 64, 128], P('grp'), parts along dimension 0
- grad_gain: float32 [256], P('grp'), parts along dimension 0
- grad_shift: float32 [256], P('grp'), parts along dimension 0
The draws below stay inside these ranges and needn't reach their ends.
There are 2 independent parts, one for each index of `grp`. The reference program is written for one: setup_inputs(seed, part) draws one part's arguments, and reference() takes and returns one part's arrays. A program takes and returns all parts, laid end to end along the dimension named above; an argument that names none is the same for every part. Nothing has to cross between parts.
All inputs are finite; a program needn't handle non-finite values.
Results may differ from the reference program's by a relative error of at most 0.0085.
Values may be sent and summed in bfloat16 or wider, within the bound.
No kernel may reach another device: no remote copies, remote signals or barrier semaphores. Data moves between devices by JAX's collectives and lax.ppermute only.
A program may use at most 64 MiB of HBM per device.

```python
import jax
import jax.numpy as jnp
from jax import lax

B = 4
CI = 64
CO = 128
YI = 64
ZI = 4
XI = 64
XO = 32
YO = 32
ZO = 2
ROWS = 128


def draw_features(key, part):
    shape = (B, XI, YI, ZI, CI)
    key_base = jax.random.fold_in(key, 11)
    key_rough = jax.random.fold_in(key, 12)
    key_offset = jax.random.fold_in(key, 13)
    base = jnp.clip(jax.random.normal(key_base, shape, jnp.float32), -4.0, 4.0)
    offset = jnp.clip(0.5 * jax.random.normal(key_offset, (CI,), jnp.float32), -1.0, 1.0)
    rough = jnp.exp(jax.random.uniform(key_rough, shape, jnp.float32, -0.7, 0.7))
    ramp = (1.0 + 2.0 * jnp.arange(XI, dtype=jnp.float32) / (XI - 1)).reshape(1, XI, 1, 1, 1)
    return ((base * rough + offset) * ramp).astype(jnp.bfloat16)


def draw_cotangent(key, part):
    shape = (ROWS, XO, ZO, CO)
    key_base = jax.random.fold_in(key, 21)
    key_rough = jax.random.fold_in(key, 22)
    base = jnp.clip(jax.random.normal(key_base, shape, jnp.float32), -4.0, 4.0)
    rough = jnp.exp(jax.random.uniform(key_rough, shape, jnp.float32, -0.7, 0.7))
    ramp = (1.0 + 2.0 * jnp.arange(XO, dtype=jnp.float32) / (XO - 1)).reshape(1, XO, 1, 1)
    return (base * rough * ramp).astype(jnp.bfloat16)


def scatter_about(stream_key, shape, spread, most, kind=jnp.bfloat16):
    array = jax.random.normal(stream_key, shape, jnp.float32) * spread
    return jnp.minimum(jnp.maximum(array, -most), most).astype(kind)


def setup_inputs(seed: int = 0, part: int = 0) -> dict:
    streams_of = jax.random.split(jax.random.key(seed), 6)
    part_keys = jax.random.split(jax.random.fold_in(streams_of[5], part), 6)
    return {
        "features": draw_features(jax.random.fold_in(jax.random.fold_in(streams_of[5], part), 71), part),
        "weight": scatter_about(streams_of[1], (3, 3, 3, CI, CO), (27 * CI) ** -0.5, 0.15625),
        "gain": jnp.clip(1.0 + 0.18 * jax.random.normal(streams_of[2], (CO,), jnp.float32), 0.1, 1.9),
        "shift": scatter_about(streams_of[3], (CO,), 0.5, 3.0, jnp.float32),
        "cotangent": draw_cotangent(jax.random.fold_in(jax.random.fold_in(streams_of[5], part), 71), part),
    }


epsilon = 1e-05
leak_slope = 0.1

def strided_conv(volume, kernel):
    return lax.conv_general_dilated(volume, kernel, (2, 2, 2), ((1, 0), (1, 0), (1, 0)), dimension_numbers=('NDHWC', 'DHWIO', 'NDHWC'), precision=lax.Precision.HIGHEST)

def reference(features, weight, gain, shift, cotangent):
    volume = features.astype(jnp.float32)
    kernel = weight.astype(jnp.float32)
    preact, pullback = jax.vjp(strided_conv, volume, kernel)
    center = lax.optimization_barrier(jnp.mean(preact, axis=(0, 1, 2, 3)))
    variance = lax.optimization_barrier(jnp.mean((preact - center) ** 2, axis=(0, 1, 2, 3)))
    inv_std = lax.rsqrt(variance + epsilon)
    unit = (preact - center) * inv_std
    normed = gain * unit + shift
    activated = jnp.where(normed >= 0, normed, leak_slope * normed).astype(jnp.bfloat16)
    regrouped = activated.transpose(0, 2, 1, 3, 4).reshape(ROWS, XO, ZO, CO)
    incoming = cotangent.reshape(B, YO, XO, ZO, CO).transpose(0, 2, 1, 3, 4).astype(jnp.float32)
    grad_act = incoming * jnp.where(normed >= 0, 1.0, leak_slope)
    grad_shift = lax.optimization_barrier(jnp.sum(grad_act, axis=(0, 1, 2, 3)))
    grad_gain = lax.optimization_barrier(jnp.sum(grad_act * unit, axis=(0, 1, 2, 3)))
    total_count = B * XO * YO * ZO
    grad_pre = (gain * inv_std * (grad_act - grad_shift / total_count - unit * grad_gain / total_count)).astype(jnp.bfloat16)
    grad_volume, grad_kernel = pullback(grad_pre.astype(jnp.float32))
    return (regrouped, grad_volume.astype(jnp.bfloat16), grad_kernel, grad_gain, grad_shift)
```

```python
import functools

import jax
import jax.numpy as jnp
from jax import lax
from jax.experimental import pallas as pl
from jax.experimental.pallas import tpu as pltpu
from jax.sharding import PartitionSpec as P

epsilon = 1e-05
leak_slope = 0.1
f32 = jnp.float32
bf16 = jnp.bfloat16
VMEM = pl.BlockSpec(memory_space=pltpu.VMEM)


def call(kernel, outs, *args, scratch=(), aliases={}, flops=0):
    moved = sum(a.size * a.dtype.itemsize for a in args) + sum(
        o.size * o.dtype.itemsize for o in outs
    )
    return pl.pallas_call(
        kernel,
        out_shape=tuple(outs),
        in_specs=[VMEM] * len(args),
        out_specs=tuple([VMEM] * len(outs)),
        scratch_shapes=list(scratch),
        input_output_aliases=aliases,
        cost_estimate=pl.CostEstimate(flops=flops, bytes_accessed=moved, transcendentals=0),
        compiler_params=pltpu.CompilerParams(vmem_limit_bytes=24 * 1024 * 1024),
    )(*args)


def shape(dims, dtype):
    return jax.ShapeDtypeStruct(tuple(dims), dtype)


def from_behind(value, axis, steps):
    count = lax.axis_size(axis)
    leading, last = (max(0, -steps), min(count, count - steps))
    return lax.ppermute(value, axis, [(source, source + steps) for source in range(leading, last)])


def build_weight(w_ref, wm_ref, tap_x, slot, size_z, chans, outc):
    out_z = size_z // 2
    for tap_y in range(3):
        for z in range(size_z):
            for q in range(out_z):
                tap_z = z - 2 * q + 1
                rows = pl.ds((tap_y * size_z + z) * chans, chans)
                lanes = pl.ds(q * outc, outc)
                if 0 <= tap_z < 3:
                    wm_ref[slot, rows, lanes] = w_ref[(tap_x * 3 + tap_y) * 3 + tap_z]
                else:
                    wm_ref[slot, rows, lanes] = jnp.zeros((chans, outc), wm_ref.dtype)


def pack_plane(plane, stage_ref, base, size_y, size_z, chans, store):
    out_y = size_y // 2
    step = 2 * size_z
    wide = plane.astype(f32)
    stage_ref[pl.ds(base, step), :] = jnp.zeros((step, 2 * chans), f32)
    stage_ref[pl.ds(base + step, size_y * size_z), :] = jnp.concatenate([wide, wide], axis=1)
    low = lax.broadcasted_iota(jnp.int32, (out_y, 2 * chans), 1) < chans
    for tap_y in range(3):
        for z in range(0, size_z, 2):
            start = base + step + (tap_y - 1) * size_z + z
            here = stage_ref[pl.ds(start, out_y, stride=step), :]
            later = stage_ref[pl.ds(start + 1, out_y, stride=step), :]
            lane = (tap_y * size_z + z) * chans
            store(lane, jnp.where(low, here, later).astype(bf16))


def forward_kernel(f_ref, w_ref, xe_ref, xo_ref, pre_ref, stage_ref, wm_ref, *, size_y, size_z):
    samples, planes, _, chans = f_ref.shape
    outc = w_ref.shape[-1]
    out_y = size_y // 2
    block = samples * out_y
    region = (size_y + 2) * size_z
    for x in range(planes):
        for b in range(samples):
            target = xo_ref if x % 2 else xe_ref
            slot = (x + 1) // 2 if x % 2 else x // 2

            def store(lane, value, target=target, row=slot * block + b * out_y):
                target[pl.ds(row, out_y), pl.ds(lane, 2 * chans)] = value

            pack_plane(
                f_ref[b, x], stage_ref, (x * samples + b) * region, size_y, size_z, chans, store
            )
    for tap_x in range(3):
        build_weight(w_ref, wm_ref, tap_x, tap_x, size_z, chans, outc)
    out_x = planes // 2
    half = out_x * block
    mid = jnp.dot(xe_ref[...], wm_ref[1], preferred_element_type=f32)
    pre_ref[...] = mid + jnp.dot(
        xo_ref[pl.ds(block, half), :], wm_ref[2], preferred_element_type=f32
    )
    if out_x > 1:
        pre_ref[pl.ds(block, half - block), :] += jnp.dot(
            xo_ref[pl.ds(block, half - block), :], wm_ref[0], preferred_element_type=f32
        )


def split3(value):
    high = value.astype(bf16)
    rest = value - high.astype(f32)
    middle = rest.astype(bf16)
    low = (rest - middle.astype(f32)).astype(bf16)
    return [high.astype(f32), middle.astype(f32), low.astype(f32)]


def stats_rows(first, second):
    rows = split3(first) + split3(second)
    rows += [jnp.zeros_like(first)] * 2
    return jnp.concatenate(rows, axis=0).astype(bf16)


def fold(value, outc):
    total = value[:, :outc]
    for q in range(1, value.shape[1] // outc):
        total = total + value[:, q * outc : (q + 1) * outc]
    return total


def tile_lanes(value, times):
    return jnp.concatenate([value] * times, axis=1)


def halo_kernel(
    h_ref, w_ref, cot_ref, xin_ref, prein_ref, xo_ref, pre_ref, pay_ref, stage_ref, wm_ref, *, size_y, size_z
):
    samples, _, chans = h_ref.shape
    outc = w_ref.shape[-1]
    out_y = size_y // 2
    block = samples * out_y
    out_z = size_z // 2
    region = (size_y + 2) * size_z
    for b in range(samples):

        def store(lane, value, row=b * out_y):
            xo_ref[pl.ds(row, out_y), pl.ds(lane, 2 * chans)] = value

        pack_plane(h_ref[b], stage_ref, b * region, size_y, size_z, chans, store)
    build_weight(w_ref, wm_ref, 0, 0, size_z, chans, outc)
    pre_ref[pl.ds(0, block), :] = prein_ref[pl.ds(0, block), :] + jnp.dot(
        xo_ref[pl.ds(0, block), :], wm_ref[0], preferred_element_type=f32
    )
    value = pre_ref[...]
    count = value.shape[0] * out_z
    mean = fold(jnp.sum(value, axis=0, keepdims=True), outc) / count
    centered = value - tile_lanes(mean, out_z)
    spread = fold(jnp.sum(centered * centered, axis=0, keepdims=True), outc)
    rows, owners, group, _ = cot_ref.shape
    stats = stats_rows(mean, spread)
    for r in range(rows):
        pay_ref[:, r] = cot_ref[r]
    for g in range(2):
        pay_ref[:, rows + g] = jnp.broadcast_to(
            stats[None, g * group : (g + 1) * group], (owners, group, outc)
        )


def norm_kernel(
    got_ref, pre_ref, gain_ref, shift_ref, unit_ref, act_ref, pay_ref, stage_ref, *, block, out_x, out_z
):
    outc = gain_ref.shape[-1]
    count, span, _ = got_ref.shape
    body = span - 8
    group = out_x * out_z
    for s in range(count):
        stage_ref[pl.ds(s * body, body), :] = got_ref[s, pl.ds(0, body), :].astype(f32)
    stats = got_ref[:, pl.ds(body, 8), :].astype(f32)
    means = stats[:, 0:1] + stats[:, 1:2] + stats[:, 2:3]
    spreads = stats[:, 3:4] + stats[:, 4:5] + stats[:, 5:6]
    center = jnp.sum(means, axis=0) / count
    local_count = block * group
    away = means - center[None]
    variance = (jnp.sum(spreads, axis=0) + local_count * jnp.sum(away * away, axis=0)) / (
        local_count * count
    )
    inv_std = lax.rsqrt(variance + epsilon)
    gain = gain_ref[...]
    shift = shift_ref[...]
    grad_shift = jnp.zeros((1, outc), f32)
    grad_gain = jnp.zeros((1, outc), f32)
    for o in range(out_x):
        for q in range(out_z):
            rows = pl.ds(o * block, block)
            lanes = pl.ds(q * outc, outc)
            strided = pl.ds(o * out_z + q, block, stride=group)
            incoming = stage_ref[strided, :]
            unit = (pre_ref[rows, lanes] - center) * inv_std
            normed = gain * unit + shift
            keep = normed >= 0
            stage_ref[strided, :] = jnp.where(keep, normed, leak_slope * normed)
            grad_act = incoming * jnp.where(keep, 1.0, leak_slope)
            unit_ref[rows, lanes] = unit
            act_ref[rows, lanes] = grad_act
            grad_shift += jnp.sum(grad_act, axis=0, keepdims=True)
            grad_gain += jnp.sum(grad_act * unit, axis=0, keepdims=True)
    sums = stats_rows(grad_shift, grad_gain)
    for s in range(count):
        pay_ref[s, pl.ds(0, body), :] = stage_ref[pl.ds(s * body, body), :].astype(bf16)
        pay_ref[s, pl.ds(body, 8), :] = sums
    unit_ref[pl.ds(out_x * block, 8), :] = jnp.broadcast_to(
        tile_lanes(inv_std, out_z), (8, out_z * outc)
    )


def grad_kernel(
    got_ref, unit_ref, act_ref, gain_ref, xe_ref, xo_ref, w_ref,
    pay_ref, pre_ref, halo_ref, gs_ref, gg_ref, wm_ref, *, block, out_y, out_x, size_z,
):
    outc = gain_ref.shape[-1]
    out_z = size_z // 2
    count, span, _ = got_ref.shape
    body = span - 8
    stats = jnp.sum(got_ref[:, pl.ds(body, 8), :].astype(f32), axis=0)
    grad_shift = stats[0:1] + stats[1:2] + stats[2:3]
    grad_gain = stats[3:4] + stats[4:5] + stats[5:6]
    gs_ref[...] = grad_shift
    gg_ref[...] = grad_gain
    half = out_x * block
    total = half * out_z * count
    inv_std = unit_ref[pl.ds(half, 1), :]
    wide = lambda v: tile_lanes(v, out_z)
    exact = (
        wide(gain_ref[...])
        * inv_std
        * (
            act_ref[...]
            - wide(grad_shift / total)
            - unit_ref[pl.ds(0, half), :] * wide(grad_gain / total)
        )
    )
    grad_pre = exact.astype(bf16)
    pre_ref[0] = grad_pre
    place = lax.broadcasted_iota(jnp.int32, exact.shape, 0)
    last = (place & (out_y - 1)) == out_y - 1
    pre_ref[1] = jnp.where(last, 0.0, pltpu.roll(exact, half - 1, axis=0)).astype(bf16)
    chans = w_ref.shape[1]
    contract = (((0,), (0,)), ((), ()))
    for tap_x in range(3):
        if tap_x == 1:
            columns = xe_ref[...]
        else:
            columns = xo_ref[pl.ds(block * (tap_x // 2), half), :]
        dense = lax.dot_general(columns, grad_pre, contract, preferred_element_type=f32)
        for tap_y in range(3):
            for tap_z in range(3):
                term = None
                for q in range(out_z):
                    z = 2 * q + tap_z - 1
                    if 0 <= z < size_z:
                        row = (tap_y * size_z + z) * chans
                        piece = dense[row : row + chans, q * outc : (q + 1) * outc]
                        term = piece if term is None else term + piece
                index = (tap_x * 3 + tap_y) * 3 + tap_z
                pay_ref[pl.ds(index * chans, chans), :] = term.astype(bf16)
    used = w_ref.shape[0] * chans
    if pay_ref.shape[0] > used:
        pay_ref[pl.ds(used, pay_ref.shape[0] - used), :] = jnp.zeros(
            (pay_ref.shape[0] - used, outc), bf16
        )
    build_weight(w_ref, wm_ref, 0, 0, size_z, chans, outc)
    even, odd = spread_rows(pre_ref, 0, block, wm_ref, 0, size_z, chans)
    halo_ref[0] = even.astype(bf16)
    halo_ref[1] = odd.astype(bf16)


def spread_rows(pre_ref, start, rows, wm_ref, slot, size_z, chans):
    width = size_z * chans
    here = pre_ref[0, pl.ds(start, rows), :]
    later = pre_ref[1, pl.ds(start, rows), :]

    def part(grad, tap_y):
        return lax.dot_general(
            grad,
            wm_ref[slot, pl.ds(tap_y * width, width), :],
            (((1,), (1,)), ((), ())),
            preferred_element_type=f32,
        )

    return part(here, 1), part(here, 2) + part(later, 0)


def input_kernel(
    pre_ref, w_ref, halo_ref, got_ref, gf_ref, rg_ref, stage_ref, wm_ref, *, block, out_y, out_x, size_z
):
    chans = w_ref.shape[1]
    outc = w_ref.shape[2]
    samples, planes, _, _ = gf_ref.shape
    half = out_x * block
    step = 2 * size_z
    for tap_x in range(3):
        build_weight(w_ref, wm_ref, tap_x, tap_x, size_z, chans, outc)
    centre = spread_rows(pre_ref, 0, half, wm_ref, 1, size_z, chans)
    after = spread_rows(pre_ref, 0, half, wm_ref, 2, size_z, chans)
    if out_x > 1:
        before = spread_rows(pre_ref, block, half - block, wm_ref, 0, size_z, chans)
    region = out_y * step
    for x in range(planes):
        o = x // 2
        for parity in range(2):
            if x % 2 == 0:
                value = centre[parity][o * block : (o + 1) * block]
            else:
                value = after[parity][o * block : (o + 1) * block]
                if o + 1 < out_x:
                    value = value + before[parity][o * block : (o + 1) * block]
                else:
                    value = value + halo_ref[parity].astype(f32)
            for b in range(samples):
                base = (x * samples + b) * region + parity * size_z
                for z in range(0, size_z, 2):
                    pair = value[b * out_y : (b + 1) * out_y, z * chans : (z + 2) * chans]
                    stage_ref[pl.ds(base + z, out_y, stride=step), :] = pair
                    stage_ref[pl.ds(base + z + 1, out_y, stride=step), :] = pltpu.roll(
                        pair, chans, axis=1
                    )
        for b in range(samples):
            base = (x * samples + b) * region
            gf_ref[b, x] = stage_ref[pl.ds(base, region), :][:, :chans].astype(bf16)
    for r in range(rg_ref.shape[0]):
        rg_ref[r] = got_ref[:, r]


def sum_kernel(got_ref, out_ref):
    count = got_ref.shape[0]
    total = got_ref[0].astype(f32)
    for s in range(1, count):
        total = total + got_ref[s].astype(f32)
    rounded = total.astype(bf16)
    for s in range(count):
        out_ref[s] = rounded


def local(features, weight, gain, shift, cotangent):
    samples, planes, size_y, size_z, chans = features.shape
    out_x, out_y, out_z = planes // 2, size_y // 2, size_z // 2
    outc = weight.shape[-1]
    count = lax.axis_size("sx")
    rows = cotangent.shape[0]
    group = out_x * out_z
    block = samples * out_y
    half = out_x * block
    width = 3 * size_z * chans
    taps = weight.reshape(27, chans, outc)
    flat = features.reshape(samples, planes, size_y * size_z, chans)
    gain_row = gain.reshape(1, outc)
    shift_row = shift.reshape(1, outc)
    region = (size_y + 2) * size_z
    muls = 2 * half * width * out_z * outc

    borrowed = from_behind(flat[:, planes - 1], "sx", 1)
    even_cols, odd_cols, partial = call(
        functools.partial(forward_kernel, size_y=size_y, size_z=size_z),
        [
            shape((half, width), bf16),
            shape((half + block, width), bf16),
            shape((half, out_z * outc), f32),
        ],
        flat,
        taps,
        scratch=[
            pltpu.VMEM((planes * samples * region, 2 * chans), f32),
            pltpu.VMEM((3, width, out_z * outc), bf16),
        ],
        flops=3 * muls,
    )
    span = rows + 8 // group
    cells = cotangent.reshape(rows, count, group, outc)
    odd_cols, preact, payload = call(
        functools.partial(halo_kernel, size_y=size_y, size_z=size_z),
        [
            shape((half + block, width), bf16),
            shape((half, out_z * outc), f32),
            shape((count, span, group, outc), bf16),
        ],
        borrowed,
        taps,
        cells,
        odd_cols,
        partial,
        scratch=[
            pltpu.VMEM((samples * region, 2 * chans), f32),
            pltpu.VMEM((1, width, out_z * outc), bf16),
        ],
        aliases={3: 0, 4: 1},
        flops=muls // out_x,
    )
    got = lax.all_to_all(payload, "sx", split_axis=0, concat_axis=0, tiled=True)
    unit, grad_act, payload = call(
        functools.partial(norm_kernel, block=block, out_x=out_x, out_z=out_z),
        [
            shape((half + 8, out_z * outc), f32),
            shape((half, out_z * outc), f32),
            shape((count, span * group, outc), bf16),
        ],
        got.reshape(count, span * group, outc),
        preact,
        gain_row,
        shift_row,
        scratch=[pltpu.VMEM((count * rows * group, outc), f32)],
        flops=muls // 64,
    )
    got = lax.all_to_all(payload, "sx", split_axis=0, concat_axis=0, tiled=True)
    share = -(-27 * chans // (count * 16)) * 16
    terms, grad_pre, halo, grad_shift, grad_gain = call(
        functools.partial(grad_kernel, block=block, out_y=out_y, out_x=out_x, size_z=size_z),
        [
            shape((count * share, outc), bf16),
            shape((2, half, out_z * outc), bf16),
            shape((2, block, size_z * chans), bf16),
            shape((1, outc), f32),
            shape((1, outc), f32),
        ],
        got,
        unit,
        grad_act,
        gain_row,
        even_cols,
        odd_cols,
        taps,
        scratch=[pltpu.VMEM((1, width, out_z * outc), bf16)],
        flops=4 * muls,
    )
    shares = lax.all_to_all(
        terms.reshape(count, share, outc), "sx", split_axis=0, concat_axis=0, tiled=True
    )
    halo = from_behind(halo, "sx", -1)
    grad_features, regrouped = call(
        functools.partial(input_kernel, block=block, out_y=out_y, out_x=out_x, size_z=size_z),
        [
            shape((samples, planes, size_y * size_z, chans), bf16),
            shape((rows, count, group, outc), bf16),
        ],
        grad_pre,
        taps,
        halo,
        got.reshape(count, span, group, outc),
        scratch=[
            pltpu.VMEM((planes * samples * size_y * size_z, 2 * chans), f32),
            pltpu.VMEM((3, width, out_z * outc), bf16),
        ],
        flops=3 * muls,
    )
    (sums,) = call(sum_kernel, [shape((count, share, outc), bf16)], shares)
    whole = lax.all_to_all(sums, "sx", split_axis=0, concat_axis=0, tiled=True)
    grad_weight = (
        whole.reshape(count * share, outc)[: 27 * chans].astype(f32).reshape(weight.shape)
    )
    return (
        regrouped.reshape(rows, count * out_x, out_z, outc),
        grad_features.reshape(features.shape),
        grad_weight,
        grad_gain.reshape(outc),
        grad_shift.reshape(outc),
    )


def solution(mesh):
    return jax.shard_map(
        local,
        mesh=mesh,
        in_specs=(
            P("grp", "sx", None, None, None),
            P(),
            P(),
            P(),
            P(("grp", "sx"), None, None, None),
        ),
        out_specs=(
            P(("grp", "sx"), None, None, None),
            P("grp", "sx", None, None, None),
            P("grp", None, None, None, None),
            P("grp"),
            P("grp"),
        ),
        check_vma=False,
    )
```
